32 devices in a mesh: dom: 8 (over y, x, core), sub: 4 (over z).
Axes of the slice: x: 2, y: 2, z: 4, core: 2. Of those that a mesh axis runs over, the one named last changes fastest.
Arguments:
- dofs: float32 [56, 9, 4096], P(None, None, ('dom', 'sub')), may hold values from -6 to 6
- star: float32 [3, 9, 9, 4096], P(None, None, None, ('dom', 'sub')), may hold values from -2 to 2
- flux_own: float32 [4, 9, 9, 4096], P(None, None, None, ('dom', 'sub')), may hold values from -2 to 2
- flux_nbr: float32 [4, 9, 9, 4096], P(None, None, None, ('dom', 'sub')), may hold values from -2 to 2
- cohesion: float32 [4096], P(('dom', 'sub')), may hold values from 0.5 to 8
- cluster: int32 [4096], P(('dom', 'sub')), may hold values from 0 to 1, as said below
- face_source: int32 [4, 4096], P(None, ('dom', 'sub')), may hold values from 0 to 607, as said below
- orient: int32 [4, 4096], P(None, ('dom', 'sub')), may hold values from 0 to 2
- send_rows: int32 [8, 4, 3, 4, 8], P('dom', 'sub'), may hold values from 0 to 511
- stiffness: float32 [3, 56, 56], replicated, may hold values from -0.75 to 0.75
- project: float32 [4, 21, 56], replicated, may hold values from -0.75 to 0.75
- lift: float32 [4, 56, 21], replicated, may hold values from -0.625 to 0.625
- rotate: float32 [3, 21, 21], replicated, may hold values from -1.25 to 1.25
Outputs:
- evolved: float32 [56, 9, 4096], P(None, None, ('dom', 'sub'))
The draws below stay inside these ranges and needn't reach their ends.
Inputs may be any that keep to these rules, and one draw needn't show every extreme that they name: 0 marks an element of the fine cluster (two steps of 0.5), 1 one of the coarse cluster (one step of 1). The share of fine elements differs from device to device. `face_source`: values below 512 name one of the device's own faces (face times 128 plus element); the value 4 * 128 + q names received row q, q = (direction * 4 + sender sub index) * 8 + slot. Of the 8 slots of every sender the last 1 to 8 are named, each by exactly one face of the device, and all 8 for at least one sender of every device.
All inputs are finite; a program needn't handle non-finite values.
Results may differ from the reference program's by a relative error of at most 0.0003.
Values sent between devices are 32-bit elements; how exact they have to be, the bound alone decides.
A program may use at most 64 MiB of HBM per device.

```python
import math
import jax
import jax.numpy as jnp
from jax import lax

B = 56
F = 21
Q = 9
ORDER = 6
E_DEV = 128
SLOTS = 8
DOMS = 8
SUBS = 4
ELEMS = 4096


def draw_cluster(key, part):
    key_one, key_two = jax.random.split(jax.random.fold_in(key, 11))
    fine_share = jax.random.randint(key_one, (DOMS * SUBS, 1), 1, 10)
    throws = jax.random.randint(key_two, (DOMS * SUBS, E_DEV), 0, 10)
    return (throws >= fine_share).astype(jnp.int32).reshape(-1)


def source_device(dev_key):
    key_one, key_two, key_three, key_four = jax.random.split(dev_key, 4)
    senders = 3 * SUBS
    faces = 4 * E_DEV
    counts = jax.random.randint(key_one, (senders,), 1, SLOTS + 1)
    filled = jax.random.randint(key_two, (), 0, senders)
    counts = jnp.where(jnp.arange(senders, dtype=jnp.int32) == filled, SLOTS, counts)
    slot_ids = jnp.arange(senders * SLOTS, dtype=jnp.int32)
    is_live = slot_ids % SLOTS >= SLOTS - counts[slot_ids // SLOTS]
    ranked = jnp.argsort(jnp.where(is_live, slot_ids, slot_ids + senders * SLOTS)).astype(jnp.int32)
    live_count = jnp.sum(is_live.astype(jnp.int32))
    position = jnp.arange(faces, dtype=jnp.int32)
    remote = faces + ranked[jnp.minimum(position, senders * SLOTS - 1)]
    own_rows = jax.random.randint(key_three, (faces,), 0, faces)
    by_position = jnp.where(position < live_count, remote, own_rows).astype(jnp.int32)
    shuffle = jax.random.permutation(key_four, faces)
    placed = jnp.zeros((faces,), jnp.int32).at[shuffle].set(by_position)
    return placed.reshape(4, E_DEV)


def draw_face_source(key, part):
    dev_keys = jax.random.split(jax.random.fold_in(key, 23), DOMS * SUBS)
    sources = jax.vmap(source_device)(dev_keys)
    return jnp.transpose(sources, (1, 0, 2)).reshape(4, DOMS * SUBS * E_DEV)


def plant(values, stream_key, least, top_value):
    longest = values.shape.index(max(values.shape))
    spots = []
    for shift in (0, 1):
        where = [jax.random.randint(jax.random.fold_in(stream_key, axis), (), 0, length) for axis, length in enumerate(values.shape)]
        where[longest] = (where[longest] + shift) % values.shape[longest]
        spots.append(tuple(where))
    return values.at[spots[0]].set(least).at[spots[1]].set(top_value)


def steps_of(key, extent, cuts, least, top_value):
    factor_of, own = 1.0, jax.random.fold_in(key, 6)
    for dim, blocks in cuts:
        heights = jnp.exp(jax.random.uniform(jax.random.fold_in(own, dim), (blocks,), jnp.float32, least / len(cuts), top_value / len(cuts)))
        factor_of = factor_of * jnp.repeat(heights, extent[dim] // blocks).reshape([-1 if axis == dim else 1 for axis in range(len(extent))])
    return factor_of


def scatter_about(rng, dims, spread, most, pieces=(), held_as=jnp.bfloat16):
    loudness = steps_of(rng, dims, pieces, -0.22, 0.18) if pieces else 1.0
    entries = jax.random.normal(rng, dims, jnp.float32) * spread * loudness
    return jnp.minimum(jnp.maximum(entries, -most), most).astype(held_as)


def setup_inputs(seed: int = 0) -> dict:
    key_list = jax.random.split(jax.random.key(seed), 14)
    return {
        "dofs": scatter_about(key_list[0], (B, Q, ELEMS), 1.0, 6.0, ((2, 32),), jnp.float32),
        "star": scatter_about(key_list[1], (3, Q, Q, ELEMS), Q ** -0.5, 2.0, ((3, 32),), jnp.float32),
        "flux_own": scatter_about(key_list[2], (4, Q, Q, ELEMS), Q ** -0.5, 2.0, ((3, 32),), jnp.float32),
        "flux_nbr": scatter_about(key_list[3], (4, Q, Q, ELEMS), Q ** -0.5, 2.0, ((3, 32),), jnp.float32),
        "cohesion": jnp.clip(jnp.exp(math.log(8.0) - 2.7725887 * jax.random.uniform(key_list[4], (ELEMS,), jnp.float32) ** steps_of(key_list[4], (ELEMS,), ((0, 32),), -0.2, 0.2)), 0.5, 8.0),
        "cluster": draw_cluster(jax.random.fold_in(key_list[13], 71), 0),
        "face_source": draw_face_source(jax.random.fold_in(key_list[13], 71), 0),
        "orient": plant(jax.random.randint(key_list[7], (4, ELEMS), 0, 3), jax.random.fold_in(key_list[7], 1), 0, 2).astype(jnp.int32),
        "send_rows": plant(jax.random.randint(key_list[8], (DOMS, SUBS, 3, SUBS, SLOTS), 0, 4 * E_DEV), jax.random.fold_in(key_list[8], 1), 0, (4 * E_DEV) - 1).astype(jnp.int32),
        "stiffness": scatter_about(key_list[9], (3, B, B), B ** -0.5, 0.75, (), jnp.float32),
        "project": scatter_about(key_list[10], (4, F, B), B ** -0.5, 0.75, (), jnp.float32),
        "lift": scatter_about(key_list[11], (4, B, F), (4 * F) ** -0.5, 0.625, (), jnp.float32),
        "rotate": scatter_about(key_list[12], (3, F, F), F ** -0.5, 1.25, (), jnp.float32),
    }


step_time = 0.5
relax_time = 0.5
highest = lax.Precision.HIGHEST

def stiff_apply(stacked, field, star):
    nbasis, nquant, elements = field.shape
    product = jnp.dot(stacked, field.reshape(nbasis, nquant * elements), precision=highest, preferred_element_type=jnp.float32)
    product = product.reshape(3, nbasis, nquant, elements)
    return jnp.einsum('dbpe,dpqe->bqe', product, star, precision=highest)

def taylor_series(stacked, field, star):
    series = [field]
    for degree in range(ORDER - 1):
        series.append(-stiff_apply(stacked, series[-1], star))
    return series

def time_integral(series, begin_time, end_time):
    summed = series[0] * (end_time - begin_time)
    for degree in range(1, ORDER):
        weight_now = (end_time ** (degree + 1) - begin_time ** (degree + 1)) / math.factorial(degree + 1)
        summed = summed + series[degree] * weight_now
    return summed

def face_table(integral, project):
    nbasis, nquant, elements = integral.shape
    face_basis = project.shape[1]
    traced = jnp.dot(project.reshape(-1, nbasis), integral.reshape(nbasis, -1), precision=highest, preferred_element_type=jnp.float32)
    traced = traced.reshape(4, face_basis, nquant, elements)
    return jnp.transpose(traced, (0, 3, 1, 2)).reshape(4 * elements, face_basis * nquant)

def table_faces(table, face_basis, nquant):
    elements = table.shape[0] // 4
    return jnp.transpose(table.reshape(4, elements, face_basis, nquant), (0, 2, 3, 1))

def neighbour_traces(table, received, face_source, orient, rotate):
    face_basis = rotate.shape[1]
    nquant = table.shape[1] // face_basis
    source = jnp.concatenate([table, received.reshape(-1, table.shape[1])], axis=0)
    picked = source[face_source.reshape(-1)].reshape(-1, face_basis, nquant)
    turned = jnp.einsum('hgk,nkq->nhgq', rotate, picked, precision=highest)
    onehot = (orient.reshape(-1)[:, None] == jnp.arange(3, dtype=jnp.int32)[None, :]).astype(jnp.float32)
    chosen = jnp.einsum('nhgq,nh->ngq', turned, onehot, precision=highest)
    return table_faces(chosen.reshape(picked.shape[0], -1), face_basis, nquant)

def face_flux(own_faces, other_faces, flux_own, flux_nbr, lift):
    terms = jnp.einsum('fgpe,fpqe->fgqe', own_faces, flux_own, precision=highest)
    terms = terms + jnp.einsum('fgpe,fpqe->fgqe', other_faces, flux_nbr, precision=highest)
    nfaces, face_basis, nquant, elements = terms.shape
    lift_flat = jnp.transpose(lift, (1, 0, 2)).reshape(lift.shape[1], -1)
    lifted = jnp.dot(lift_flat, terms.reshape(nfaces * face_basis, -1), precision=highest, preferred_element_type=jnp.float32)
    return lifted.reshape(lift.shape[1], nquant, elements)

def plastic_return(field, cohesion, relax):
    stress = field[0, 0:6, :]
    pressure = (stress[0] + stress[1] + stress[2]) / 3.0
    dev_x = stress[0] - pressure
    dev_y = stress[1] - pressure
    dev_z = stress[2] - pressure
    second_inv = 0.5 * (dev_x * dev_x + dev_y * dev_y + dev_z * dev_z) + stress[3] * stress[3] + stress[4] * stress[4] + stress[5] * stress[5]
    strength = jnp.sqrt(second_inv)
    factor = 1.0 - (1.0 - cohesion / jnp.maximum(strength, cohesion)) * relax
    normal = field[:, 0:3, :]
    mode_mean = (normal[:, 0:1, :] + normal[:, 1:2, :] + normal[:, 2:3, :]) / 3.0
    normal = mode_mean + factor * (normal - mode_mean)
    shear = factor * field[:, 3:6, :]
    return jnp.concatenate([normal, shear, field[:, 6:, :]], axis=1)

def route(tables, send_rows):
    width = tables.shape[-1]
    rows_out = jnp.take_along_axis(tables, send_rows.reshape(DOMS * SUBS, -1)[:, :, None], axis=1)
    outgoing = rows_out.reshape(DOMS, SUBS, 3, SUBS, SLOTS, width)
    from_below = jnp.roll(outgoing[:, :, 2], 1, axis=0)
    same_slab = outgoing[:, :, 1]
    from_above = jnp.roll(outgoing[:, :, 0], -1, axis=0)
    stacked = jnp.stack([from_below, same_slab, from_above], axis=2)
    arranged = jnp.transpose(stacked, (0, 3, 2, 1, 4, 5))
    return arranged.reshape(DOMS * SUBS, 3 * SUBS * SLOTS, width)

def reference(dofs, star, flux_own, flux_nbr, cohesion, cluster, face_source, orient, send_rows, stiffness, project, lift, rotate):
    devices = DOMS * SUBS

    def split(array):
        return jnp.moveaxis(array.reshape(array.shape[:-1] + (devices, E_DEV)), -2, 0)
    deriv_stack = stiffness.reshape(-1, B)
    volume_stack = jnp.transpose(stiffness, (0, 2, 1)).reshape(-1, B)
    fine_relax = 1.0 - math.exp(-step_time / relax_time)
    coarse_relax = 1.0 - math.exp(-2.0 * step_time / relax_time)
    dofs_dev = split(dofs)
    star_dev = split(star)
    own_dev = split(flux_own)
    nbr_dev = split(flux_nbr)
    coh_dev = split(cohesion)
    clus_dev = split(cluster)
    src_dev = split(face_source)
    ori_dev = split(orient)

    def phase_one(items):
        field, star_here = items
        series = taylor_series(deriv_stack, field, star_here)
        first = time_integral(series, 0.0, step_time)
        second_coarse = time_integral(series, step_time, 2.0 * step_time)
        return (first, second_coarse, face_table(first, project))
    first, second_coarse, table_one = lax.map(phase_one, (dofs_dev, star_dev))
    received_one = route(table_one, send_rows)

    def phase_two(items):
        field, star_here, own_here, nbr_here, coh_here, clus_here, src_here, ori_here, first_here, coarse_here, tab_here, recv_here = items
        own_one = table_faces(tab_here, F, Q)
        other_one = neighbour_traces(tab_here, recv_here, src_here, ori_here, rotate)
        update = field + stiff_apply(volume_stack, first_here, star_here) - face_flux(own_one, other_one, own_here, nbr_here, lift)
        stepped = plastic_return(update, coh_here, fine_relax)
        series = taylor_series(deriv_stack, stepped, star_here)
        fine_second = time_integral(series, 0.0, step_time)
        second = jnp.where(clus_here[None, None, :] == 0, fine_second, coarse_here)
        return (stepped, second, face_table(second, project), other_one)
    stepped, second, table_two, other_one = lax.map(phase_two, (dofs_dev, star_dev, own_dev, nbr_dev, coh_dev, clus_dev, src_dev, ori_dev, first, second_coarse, table_one, received_one))
    received_two = route(table_two, send_rows)

    def phase_three(items):
        field, star_here, own_here, nbr_here, coh_here, clus_here, src_here, ori_here, first_here, second_here, stepped_here, tab_one, tab_two, recv_two, other_first = items
        own_one = table_faces(tab_one, F, Q)
        own_two = table_faces(tab_two, F, Q)
        other_two = neighbour_traces(tab_two, recv_two, src_here, ori_here, rotate)
        fine_update = stepped_here + stiff_apply(volume_stack, second_here, star_here) - face_flux(own_two, other_two, own_here, nbr_here, lift)
        fine_final = plastic_return(fine_update, coh_here, fine_relax)
        coarse_update = field + stiff_apply(volume_stack, first_here + second_here, star_here) - face_flux(own_one + own_two, other_first + other_two, own_here, nbr_here, lift)
        coarse_final = plastic_return(coarse_update, coh_here, coarse_relax)
        return jnp.where(clus_here[None, None, :] == 0, fine_final, coarse_final)
    result = lax.map(phase_three, (dofs_dev, star_dev, own_dev, nbr_dev, coh_dev, clus_dev, src_dev, ori_dev, first, second, stepped, table_one, table_two, received_two, other_one))
    return jnp.moveaxis(result, 0, -2).reshape(B, Q, devices * E_DEV)
```

```python
import functools
import math

import jax
import jax.numpy as jnp
from jax import lax
from jax.experimental import pallas as pl
from jax.experimental.pallas import tpu as pltpu
from jax.sharding import PartitionSpec as P

ORDER = 6
step_time = 0.5
relax_time = 0.5
f32 = jnp.float32
bf16 = jnp.bfloat16
MESH = pl.DeviceIdType.MESH


def series_weights():
    first, second = [], []
    for k in range(ORDER):
        sign = (-1.0) ** k / math.factorial(k + 1)
        low, high = step_time ** (k + 1), (2.0 * step_time) ** (k + 1)
        first.append(sign * low)
        second.append(sign * (high - low))
    return first + second


def round_up(n, m):
    return -(-n // m) * m


def parts(x):
    high = x.astype(bf16).astype(f32)
    return high, x - high


def split_rows(x):
    high = x.astype(bf16)
    return high, (x - high.astype(f32)).astype(bf16)


def kernel(dims, *refs):
    count = 13
    loaded = refs[count + 1 : 2 * count + 1]
    body(dims, refs[:count], loaded, refs[-1], *loaded, refs[count], *refs[2 * count + 1 : -1])


def body(
    dims,
    given,
    loaded,
    load_sem,
    dofs,
    star,
    flux_own,
    flux_nbr,
    cohesion,
    cluster,
    face_source,
    orient,
    send_rows,
    stiff,
    project,
    lift,
    rotate,
    out,
    mats,
    lift_t,
    rot_s,
    send_s,
    a_mat,
    l_mat,
    r_ref,
    cat,
    prod,
    u0,
    u1,
    acc1,
    acc2,
    upd,
    tr,
    tcat,
    oh,
    pick,
    nb,
    terms,
    tcat3,
    send,
    recv,
    send_sem,
    recv_sem,
):
    nb_, nq, ne, nf, nsub, ndom, bp, gp, npd = dims
    rows = 3 * nb_
    nrecv = 3 * nsub * 8
    dom, sub = lax.axis_index("dom"), lax.axis_index("sub")

    def peer(direction, k):
        return (
            lax.rem(dom + direction - 1 + ndom, ndom),
            lax.rem(sub + k, nsub),
        )

    links = [(d, k) for d in range(3) for k in range(nsub) if not (d == 1 and k == 0)]
    low = 1 - (2 * sub) // nsub
    far_first = []
    for r in range(nsub):
        place = low * (nsub - 1 - 2 * r) + r
        apart = lax.rem(place - sub + nsub, nsub)
        far_first += [(0, apart), (2, apart)]
        if r + 1 < nsub:
            far_first.append((1, low * (nsub - 2 * (r + 1)) + r + 1))
    barrier = pltpu.get_barrier_semaphore()
    for d, k in links:
        pl.semaphore_signal(barrier, inc=1, device_id=peer(d, k), device_id_type=MESH)

    loads = [
        pltpu.make_async_copy(source, place, load_sem.at[n])
        for n, (source, place) in enumerate(zip(given, loaded))
    ]
    early = (0, 1, 8, 9, 10)
    for n in list(early) + [n for n in range(len(loads)) if n not in early]:
        loads[n].start()

    def lanes(q):
        return slice(q * ne, (q + 1) * ne)

    pad_rows = jnp.zeros((bp - nb_, ne), f32)

    def put_cat(q, x):
        high, low = split_rows(jnp.concatenate([x, pad_rows], axis=0))
        cat[0:bp, lanes(q)] = high
        cat[bp : 2 * bp, lanes(q)] = high
        cat[2 * bp : 3 * bp, lanes(q)] = low

    def star_mul(emit):
        for q0 in range(0, nq, 3):
            qs = range(q0, min(q0 + 3, nq))
            accs = [None] * len(qs)
            for d in range(3):
                for p in range(nq):
                    block = prod[d * nb_ : (d + 1) * nb_, lanes(p)]
                    for n, q in enumerate(qs):
                        term = block * star[p, q, d : d + 1, :]
                        accs[n] = term if accs[n] is None else accs[n] + term
            for n, q in enumerate(qs):
                emit(q, accs[n])

    wts = series_weights()

    def pick_weight(k, base):
        value = jnp.float32(wts[base + ORDER - 1])
        for n in range(1, ORDER - 1):
            value = jnp.where(k == n, jnp.float32(wts[base + n]), value)
        return value

    def mat_cat(low, high):
        return jnp.dot(a_mat[low:high, :], cat[...], preferred_element_type=f32)

    def series(second_too):
        def body(k, carry):
            prod[...] = mat_cat(0, rows)
            w1, w2 = pick_weight(k, 0), pick_weight(k, ORDER)

            def emit(q, x):
                put_cat(q, x)
                acc1[:, lanes(q)] = acc1[:, lanes(q)] + w1 * x
                if second_too:
                    acc2[:, lanes(q)] = acc2[:, lanes(q)] + w2 * x

            star_mul(emit)
            return carry

        lax.fori_loop(1, ORDER, body, 0)

    def exchange(phase):
        copies = []
        for d, k in far_first:
            target = peer(d, k)
            copies.append(
                pltpu.make_async_remote_copy(
                    src_ref=send.at[phase, d * nsub + target[1]],
                    dst_ref=recv.at[phase, (2 - d) * nsub + sub],
                    send_sem=send_sem.at[phase, d * nsub + k],
                    recv_sem=recv_sem.at[phase, (2 - d) * nsub + k],
                    device_id=target,
                    device_id_type=MESH,
                )
            )
        return copies

    def traces(phase):
        for q in range(nq):
            put_cat(q, acc1[:, lanes(q)])
        tr[...] = mat_cat(2 * rows, 2 * rows + nf * gp)
        for f in range(nf):
            own = [tr[f * gp : (f + 1) * gp, lanes(q)] for q in range(nq)]
            own.append(jnp.zeros((npd - nq * gp, ne), f32))
            high, low = split_rows(jnp.concatenate(own, axis=0))
            tcat[0:npd, lanes(f)] = high
            tcat[npd : 2 * npd, lanes(f)] = low
        spots = lax.broadcasted_iota(jnp.int32, (8, nf * ne), 1).astype(f32)
        columns = send_s[...].T
        chosen = jnp.concatenate(
            [
                jnp.where(spots == columns[:, c : c + 1], 1.0, 0.0)
                for c in range(3 * nsub)
            ],
            axis=0,
        ).astype(bf16)
        nt = (((1,), (1,)), ((), ()))
        outgoing = lax.dot_general(
            chosen, tcat[0:npd, :], nt, preferred_element_type=f32
        ) + lax.dot_general(chosen, tcat[npd : 2 * npd, :], nt, preferred_element_type=f32)
        send[phase] = outgoing.reshape(3 * nsub, 8, npd)
        if phase == 0:
            pl.semaphore_wait(barrier, len(links))
        copies = exchange(phase)
        for copy in copies:
            copy.start()
        return copies

    def volume(emit):
        prod[...] = mat_cat(rows, 2 * rows)
        star_mul(emit)

    def flux(source, matrix, first):
        for f in range(nf):
            at = slice(f * gp, (f + 1) * gp)
            if first:
                accs = [None] * nq
            else:
                accs = [terms[at, lanes(q)] for q in range(nq)]
            for p in range(nq):
                block = source[at, lanes(p)]
                for q in range(nq):
                    term = block * matrix[p, q, f : f + 1, :]
                    accs[q] = term if accs[q] is None else accs[q] + term
            for q in range(nq):
                terms[at, lanes(q)] = accs[q]

    def own_side():
        pick[...] = jnp.dot(tcat[...], oh[0 : nf * ne, :], preferred_element_type=f32)
        flux(tr, flux_own, True)

    def other_side(phase, copies):
        for copy in copies:
            copy.wait()
        recv[phase, pl.ds(nsub + sub, 1)] = send[phase, pl.ds(nsub + sub, 1)]
        arrived = recv[phase].reshape(nrecv, npd).T
        high, low = split_rows(arrived)
        far = oh[nf * ne : nf * ne + nrecv, :]
        pick[0:npd, :] = pick[0:npd, :] + jnp.dot(high, far, preferred_element_type=f32)
        pick[npd : 2 * npd, :] = pick[npd : 2 * npd, :] + jnp.dot(
            low, far, preferred_element_type=f32
        )
        r_mat = r_ref[...]
        extra = jnp.zeros((r_mat.shape[1] - 3 * gp, nf * ne), f32)
        for q in range(nq):
            high = pick[q * gp : (q + 1) * gp, :]
            low = pick[npd + q * gp : npd + (q + 1) * gp, :]
            stacked = jnp.concatenate([high, high, low, extra], axis=0).astype(bf16)
            turned = jnp.dot(r_mat, stacked, preferred_element_type=f32)
            for f in range(nf):
                code = jnp.broadcast_to(orient[f : f + 1, :], (gp, ne))
                part = turned[:, lanes(f)]
                nb[f * gp : (f + 1) * gp, lanes(q)] = jnp.where(
                    code == 0,
                    part[0:gp],
                    jnp.where(code == 1, part[gp : 2 * gp], part[2 * gp : 3 * gp]),
                )
        flux(nb, flux_nbr, False)
        high, low = split_rows(terms[...])
        ng = nf * gp
        tcat3[0:ng, :] = high
        tcat3[ng : 2 * ng, :] = high
        tcat3[2 * ng : 3 * ng, :] = low
        return jnp.dot(l_mat[...], tcat3[...], preferred_element_type=f32)

    def plastic(field, relax, emit):
        s = [field[q][0:1, :] for q in range(6)]
        pressure = (s[0] + s[1] + s[2]) / 3.0
        dx, dy, dz = s[0] - pressure, s[1] - pressure, s[2] - pressure
        inv = (
            0.5 * (dx * dx + dy * dy + dz * dz) + s[3] * s[3] + s[4] * s[4] + s[5] * s[5]
        )
        coh = cohesion[...]
        factor = 1.0 - (1.0 - coh / jnp.maximum(jnp.sqrt(inv), coh)) * relax
        mean = (field[0] + field[1] + field[2]) * (1.0 / 3.0)
        for q in range(3):
            emit(q, mean + factor * (field[q] - mean))
        for q in range(3, 6):
            emit(q, factor * field[q])
        for q in range(6, nq):
            emit(q, field[q])

    fine_relax = 1.0 - math.exp(-step_time / relax_time)
    coarse_relax = 1.0 - math.exp(-2.0 * step_time / relax_time)

    mats[...] = jnp.zeros_like(mats)
    for n in early:
        loads[n].wait()
    ng = project.shape[0]
    for d in range(3):
        mats[d * nb_ : (d + 1) * nb_, 0:nb_] = stiff[d]
        mats[rows + d * nb_ : rows + (d + 1) * nb_, 0:nb_] = stiff[d].T
    for f in range(nf):
        at = 2 * rows + f * gp
        mats[at : at + ng, 0:nb_] = project[:, f, :]
    high, low = parts(mats[...])
    a_mat[...] = jnp.concatenate([high, low, high], axis=1).astype(bf16)
    for d in range(3):
        send_s[d * nsub : (d + 1) * nsub, :] = send_rows[d].astype(f32)

    def later_constants():
        lift_t[...] = jnp.zeros_like(lift_t)
        for f in range(nf):
            lift_t[f * gp : f * gp + ng, :] = lift[:, f, :]
        high, low = parts(lift_t[...])
        l_mat[...] = jnp.concatenate([high, low, high], axis=0).T.astype(bf16)
        rot_s[...] = jnp.zeros_like(rot_s)
        for h in range(3):
            rot_s[h * gp : h * gp + ng, 0:ng] = rotate[h]
        high, low = parts(rot_s[...].T)
        blank = jnp.zeros((r_ref.shape[1] - 3 * gp, 3 * gp), f32)
        r_ref[...] = jnp.concatenate([high, low, high, blank], axis=0).T.astype(bf16)

    for q in range(nq):
        x = dofs[q]
        u0[:, lanes(q)] = x
        put_cat(q, x)
        acc1[:, lanes(q)] = wts[0] * x
        acc2[:, lanes(q)] = wts[ORDER] * x
    series(True)
    copies = traces(0)
    for n in range(len(loads)):
        if n not in early:
            loads[n].wait()
    later_constants()
    for f in range(nf):
        code = face_source[f : f + 1, :]
        for r in range(0, nf * ne + nrecv, 32):
            row = lax.broadcasted_iota(jnp.int32, (32, ne), 0) + r
            oh[r : r + 32, lanes(f)] = jnp.where(row == code, 1.0, 0.0).astype(bf16)

    def keep(q, x):
        upd[:, lanes(q)] = x

    volume(keep)
    own_side()
    lifted = other_side(0, copies)
    upd[...] = upd[...] - lifted

    def keep_stepped(q, x):
        u1[:, lanes(q)] = x
        put_cat(q, x)
        acc1[:, lanes(q)] = wts[0] * x

    plastic([u0[:, lanes(q)] + upd[:, lanes(q)] for q in range(nq)], fine_relax, keep_stepped)

    series(False)
    fine = cluster[...] == 0
    for q in range(nq):
        acc1[:, lanes(q)] = jnp.where(fine, acc1[:, lanes(q)], acc2[:, lanes(q)])
    copies = traces(1)

    def keep_second(q, x):
        at = lanes(q)
        u1[:, at] = x + jnp.where(fine, u1[:, at], u0[:, at] + upd[:, at])

    volume(keep_second)
    own_side()
    upd[...] = other_side(1, copies)

    def write(q, x):
        out[q] = x

    plastic(
        [u1[:, lanes(q)] - upd[:, lanes(q)] for q in range(nq)],
        jnp.where(fine, fine_relax, coarse_relax),
        write,
    )


def local(
    mesh,
    dofs,
    star,
    flux_own,
    flux_nbr,
    cohesion,
    cluster,
    face_source,
    orient,
    send_rows,
    stiffness,
    project,
    lift,
    rotate,
):
    nbas, nq, ne = dofs.shape
    nf, ng = project.shape[0], project.shape[1]
    nsub, ndom = mesh.shape["sub"], mesh.shape["dom"]
    bp = round_up(nbas, 16)
    gp = round_up(ng, 8)
    npd = round_up(nq * gp, 32)
    rp = round_up(3 * gp, 16)
    nrecv = 3 * nsub * 8
    dims = (nbas, nq, ne, nf, nsub, ndom, bp, gp, npd)
    vmem = pl.BlockSpec(memory_space=pltpu.VMEM)
    wide = nq * ne
    args = (
        jnp.transpose(dofs, (1, 0, 2)),
        jnp.transpose(star, (1, 2, 0, 3)),
        jnp.transpose(flux_own, (1, 2, 0, 3)),
        jnp.transpose(flux_nbr, (1, 2, 0, 3)),
        cohesion.reshape(1, ne),
        cluster.reshape(1, ne),
        face_source,
        orient,
        send_rows.reshape(send_rows.shape[2:]),
        stiffness,
        jnp.transpose(project, (1, 0, 2)),
        jnp.transpose(lift, (2, 0, 1)),
        rotate,
    )
    result = pl.pallas_call(
        functools.partial(kernel, dims),
        out_shape=pltpu.VMEM((nq, nbas, ne), f32),
        in_specs=[pl.BlockSpec(memory_space=pltpu.HBM)] * len(args),
        out_specs=vmem,
        scratch_shapes=[pltpu.VMEM(x.shape, x.dtype) for x in args]
        + [
            pltpu.VMEM((6 * nbas + nf * gp, bp), f32),
            pltpu.VMEM((nf * gp, nbas), f32),
            pltpu.VMEM((3 * gp, gp), f32),
            pltpu.VMEM((3 * nsub, 8), f32),
            pltpu.VMEM((6 * nbas + nf * gp, 3 * bp), bf16),
            pltpu.VMEM((nbas, 3 * nf * gp), bf16),
            pltpu.VMEM((3 * gp, rp), bf16),
            pltpu.VMEM((3 * bp, wide), bf16),
            pltpu.VMEM((3 * nbas, wide), f32),
            pltpu.VMEM((nbas, wide), f32),
            pltpu.VMEM((nbas, wide), f32),
            pltpu.VMEM((nbas, wide), f32),
            pltpu.VMEM((nbas, wide), f32),
            pltpu.VMEM((nbas, wide), f32),
            pltpu.VMEM((nf * gp, wide), f32),
            pltpu.VMEM((2 * npd, nf * ne), bf16),
            pltpu.VMEM((nf * ne + nrecv, nf * ne), bf16),
            pltpu.VMEM((2 * npd, nf * ne), f32),
            pltpu.VMEM((nf * gp, wide), f32),
            pltpu.VMEM((nf * gp, wide), f32),
            pltpu.VMEM((3 * nf * gp, wide), bf16),
            pltpu.VMEM((2, 3 * nsub, 8, npd), f32),
            pltpu.VMEM((2, 3 * nsub, 8, npd), f32),
            pltpu.SemaphoreType.DMA((2, 3 * nsub)),
            pltpu.SemaphoreType.DMA((2, 3 * nsub)),
            pltpu.SemaphoreType.DMA((len(args),)),
        ],
        compiler_params=pltpu.CompilerParams(
            collective_id=0, has_side_effects=True, vmem_limit_bytes=48 * 1024 * 1024
        ),
        name="window",
    )(*(pltpu.with_memory_space_constraint(x, pltpu.HBM) for x in args))
    return jnp.transpose(result, (1, 0, 2))


def solution(mesh):
    both = ("dom", "sub")
    placed = (
        P(None, None, both),
        P(None, None, None, both),
        P(None, None, None, both),
        P(None, None, None, both),
        P(both),
        P(both),
        P(None, both),
        P(None, both),
        P("dom", "sub", None, None, None),
        P(),
        P(),
        P(),
        P(),
    )
    return jax.shard_map(
        functools.partial(local, mesh),
        mesh=mesh,
        in_specs=placed,
        out_specs=P(None, None, both),
        check_vma=False,
    )
```

```python
import functools
import math

import jax
import jax.numpy as jnp
from jax import lax
from jax.experimental import pallas as pl
from jax.experimental.pallas import tpu as pltpu
from jax.sharding import PartitionSpec as P

ORDER = 6
step_time = 0.5
relax_time = 0.5
f32 = jnp.float32
bf16 = jnp.bfloat16
MESH = pl.DeviceIdType.MESH


def series_weights():
    first, second = [], []
    for k in range(ORDER):
        sign = (-1.0) ** k / math.factorial(k + 1)
        low, high = step_time ** (k + 1), (2.0 * step_time) ** (k + 1)
        first.append(sign * low)
        second.append(sign * (high - low))
    return first + second


def round_up(n, m):
    return -(-n // m) * m


def parts(x):
    high = x.astype(bf16).astype(f32)
    return high, x - high


def split_rows(x):
    high = x.astype(bf16)
    return high, (x - high.astype(f32)).astype(bf16)


def kernel(dims, *refs):
    count = 13
    loaded = refs[count + 1 : 2 * count + 1]
    body(dims, refs[:count], loaded, refs[-1], *loaded, refs[count], *refs[2 * count + 1 : -1])


def body(
    dims,
    given,
    loaded,
    load_sem,
    dofs,
    star,
    flux_own,
    flux_nbr,
    cohesion,
    cluster,
    face_source,
    orient,
    send_rows,
    stiff,
    project,
    lift,
    rotate,
    out,
    mats,
    lift_t,
    rot_s,
    send_s,
    a_mat,
    l_mat,
    r_ref,
    cat,
    prod,
    u0,
    u1,
    acc1,
    acc2,
    upd,
    tr,
    tcat,
    oh,
    far,
    flat,
    g_far,
    code_far,
    pick,
    nb,
    terms,
    tcat3,
    send,
    recv,
    send_sem,
    recv_sem,
):
    nb_, nq, ne, nf, nsub, ndom, bp, gp, npd = dims
    rows = 3 * nb_
    nrecv = 3 * nsub * 8
    rl = round_up(nrecv, 128)
    dom, sub = lax.axis_index("dom"), lax.axis_index("sub")

    def peer(direction, k):
        return (
            lax.rem(dom + direction - 1 + ndom, ndom),
            lax.rem(sub + k, nsub),
        )

    links = [(d, k) for d in range(3) for k in range(nsub) if not (d == 1 and k == 0)]
    low = 1 - (2 * sub) // nsub
    far_first = []
    for r in range(nsub):
        place = low * (nsub - 1 - 2 * r) + r
        apart = lax.rem(place - sub + nsub, nsub)
        far_first += [(0, apart), (2, apart)]
        if r + 1 < nsub:
            far_first.append((1, low * (nsub - 2 * (r + 1)) + r + 1))
    barrier = pltpu.get_barrier_semaphore()
    for d, k in links:
        pl.semaphore_signal(barrier, inc=1, device_id=peer(d, k), device_id_type=MESH)

    loads = [
        pltpu.make_async_copy(source, place, load_sem.at[n])
        for n, (source, place) in enumerate(zip(given, loaded))
    ]
    early = (0, 1, 8, 9, 10)
    for n in list(early) + [n for n in range(len(loads)) if n not in early]:
        loads[n].start()

    def lanes(q):
        return slice(q * ne, (q + 1) * ne)

    pad_rows = jnp.zeros((bp - nb_, ne), f32)

    def put_cat(q, x):
        high, low = split_rows(jnp.concatenate([x, pad_rows], axis=0))
        cat[0:bp, lanes(q)] = high
        cat[bp : 2 * bp, lanes(q)] = high
        cat[2 * bp : 3 * bp, lanes(q)] = low

    def star_mul(emit):
        for q0 in range(0, nq, 3):
            qs = range(q0, min(q0 + 3, nq))
            accs = [None] * len(qs)
            for d in range(3):
                for p in range(nq):
                    block = prod[d * nb_ : (d + 1) * nb_, lanes(p)]
                    for n, q in enumerate(qs):
                        term = block * star[p, q, d : d + 1, :]
                        accs[n] = term if accs[n] is None else accs[n] + term
            for n, q in enumerate(qs):
                emit(q, accs[n])

    wts = series_weights()

    def pick_weight(k, base):
        value = jnp.float32(wts[base + ORDER - 1])
        for n in range(1, ORDER - 1):
            value = jnp.where(k == n, jnp.float32(wts[base + n]), value)
        return value

    def mat_cat(low, high):
        return jnp.dot(a_mat[low:high, :], cat[...], preferred_element_type=f32)

    def series(second_too):
        def body(k, carry):
            prod[...] = mat_cat(0, rows)
            w1, w2 = pick_weight(k, 0), pick_weight(k, ORDER)

            def emit(q, x):
                put_cat(q, x)
                acc1[:, lanes(q)] = acc1[:, lanes(q)] + w1 * x
                if second_too:
                    acc2[:, lanes(q)] = acc2[:, lanes(q)] + w2 * x

            star_mul(emit)
            return carry

        lax.fori_loop(1, ORDER, body, 0)

    nt = (((1,), (1,)), ((), ()))

    def exchange(phase):
        copies = []
        for d, k in far_first:
            target = peer(d, k)
            copies.append(
                pltpu.make_async_remote_copy(
                    src_ref=send.at[phase, d * nsub + target[1]],
                    dst_ref=recv.at[phase, (2 - d) * nsub + sub],
                    send_sem=send_sem.at[phase, d * nsub + k],
                    recv_sem=recv_sem.at[phase, (2 - d) * nsub + k],
                    device_id=target,
                    device_id_type=MESH,
                )
            )
        return copies

    def traces(phase):
        for q in range(nq):
            put_cat(q, acc1[:, lanes(q)])
        tr[...] = mat_cat(2 * rows, 2 * rows + nf * gp)
        for f in range(nf):
            own = [tr[f * gp : (f + 1) * gp, lanes(q)] for q in range(nq)]
            own.append(jnp.zeros((npd - nq * gp, ne), f32))
            high, low = split_rows(jnp.concatenate(own, axis=0))
            tcat[0:npd, lanes(f)] = high
            tcat[npd : 2 * npd, lanes(f)] = low
        spots = lax.broadcasted_iota(jnp.int32, (8, nf * ne), 1).astype(f32)
        columns = send_s[...].T
        chosen = jnp.concatenate(
            [
                jnp.where(spots == columns[:, c : c + 1], 1.0, 0.0)
                for c in range(3 * nsub)
            ],
            axis=0,
        ).astype(bf16)
        outgoing = lax.dot_general(
            chosen, tcat[0:npd, :], nt, preferred_element_type=f32
        ) + lax.dot_general(chosen, tcat[npd : 2 * npd, :], nt, preferred_element_type=f32)
        send[phase] = outgoing.reshape(3 * nsub, 8, npd)
        if phase == 0:
            pl.semaphore_wait(barrier, len(links))
        copies = exchange(phase)
        for copy in copies:
            copy.start()
        return copies

    def volume(emit):
        prod[...] = mat_cat(rows, 2 * rows)
        star_mul(emit)

    def flux(source, matrix, first):
        for f in range(nf):
            at = slice(f * gp, (f + 1) * gp)
            if first:
                accs = [None] * nq
            else:
                accs = [terms[at, lanes(q)] for q in range(nq)]
            for p in range(nq):
                block = source[at, lanes(p)]
                for q in range(nq):
                    term = block * matrix(p, q, f)
                    accs[q] = term if accs[q] is None else accs[q] + term
            for q in range(nq):
                terms[at, lanes(q)] = accs[q]

    def own_side():
        pick[...] = jnp.dot(tcat[...], oh[...], preferred_element_type=f32)
        flux(tr, lambda p, q, f: flux_own[p, q, f : f + 1, :], True)

    def choose(turned, code, at):
        part = turned[:, at]
        return jnp.where(
            code == 0,
            part[0:gp],
            jnp.where(code == 1, part[gp : 2 * gp], part[2 * gp : 3 * gp]),
        )

    def near_side():
        r_mat = r_ref[...]
        extra = jnp.zeros((r_mat.shape[1] - 3 * gp, nf * ne), f32)
        for q in range(nq):
            high = pick[q * gp : (q + 1) * gp, :]
            low = pick[npd + q * gp : npd + (q + 1) * gp, :]
            stacked = jnp.concatenate([high, high, low, extra], axis=0).astype(bf16)
            turned = jnp.dot(r_mat, stacked, preferred_element_type=f32)
            for f in range(nf):
                code = jnp.broadcast_to(orient[f : f + 1, :], (gp, ne))
                nb[f * gp : (f + 1) * gp, lanes(q)] = choose(turned, code, lanes(f))
        flux(nb, lambda p, q, f: flux_nbr[p, q, f : f + 1, :], False)

    def far_constants():
        for p in range(nq):
            for q in range(nq):
                at = (p * nq + q) * nf
                flat[at : at + nf, :] = flux_nbr[p, q]
        total, turn = None, None
        for f in range(nf):
            hit = far[0:rl, lanes(f)]
            high, low = split_rows(flat[pl.ds(f, nq * nq, stride=nf), :])
            taken = lax.dot_general(high, hit, nt, preferred_element_type=f32)
            taken = taken + lax.dot_general(low, hit, nt, preferred_element_type=f32)
            total = taken if total is None else total + taken
            code = jnp.broadcast_to(orient[f : f + 1, :], (8, ne)).astype(f32).astype(bf16)
            taken = lax.dot_general(code, hit, nt, preferred_element_type=f32)
            turn = taken if turn is None else turn + taken
        g_far[...] = total
        code_far[...] = turn

    def other_side(phase, copies):
        for copy in copies:
            copy.wait()
        recv[phase, pl.ds(nsub + sub, 1)] = send[phase, pl.ds(nsub + sub, 1)]
        arrived = recv[phase].reshape(nrecv, npd)
        if rl > nrecv:
            arrived = jnp.concatenate([arrived, jnp.zeros((rl - nrecv, npd), f32)], axis=0)
        arrived = arrived.T
        r_mat = r_ref[...]
        wide = jnp.concatenate([arrived[q * gp : (q + 1) * gp] for q in range(nq)], axis=1)
        high, low = parts(wide)
        extra = jnp.zeros((r_mat.shape[1] - 3 * gp, nq * rl), f32)
        stacked = jnp.concatenate([high, high, low, extra], axis=0).astype(bf16)
        turned = jnp.dot(r_mat, stacked, preferred_element_type=f32)
        code = jnp.broadcast_to(code_far[0:1, :], (gp, rl))
        blocks = [choose(turned, code, slice(p * rl, (p + 1) * rl)) for p in range(nq)]
        sums = []
        for q in range(nq):
            total = None
            for p in range(nq):
                term = blocks[p] * g_far[p * nq + q : p * nq + q + 1, :]
                total = term if total is None else total + term
            sums.append(total)
        sums.append(jnp.zeros((npd - nq * gp, rl), f32))
        high, low = split_rows(jnp.concatenate(sums, axis=0))
        spread = jnp.dot(
            jnp.concatenate([high, low], axis=1), far[...], preferred_element_type=f32
        )
        ng = nf * gp
        for q in range(nq):
            whole = jnp.concatenate(
                [
                    terms[f * gp : (f + 1) * gp, lanes(q)]
                    + spread[q * gp : (q + 1) * gp, lanes(f)]
                    for f in range(nf)
                ],
                axis=0,
            )
            high, low = split_rows(whole)
            tcat3[0:ng, lanes(q)] = high
            tcat3[ng : 2 * ng, lanes(q)] = low
        both = jnp.dot(l_mat[...], tcat3[...], preferred_element_type=f32)
        return both[0:nb_] + both[nb_ : 2 * nb_]

    def plastic(field, relax, emit):
        s = [field[q][0:1, :] for q in range(6)]
        pressure = (s[0] + s[1] + s[2]) / 3.0
        dx, dy, dz = s[0] - pressure, s[1] - pressure, s[2] - pressure
        inv = (
            0.5 * (dx * dx + dy * dy + dz * dz) + s[3] * s[3] + s[4] * s[4] + s[5] * s[5]
        )
        coh = cohesion[...]
        factor = 1.0 - (1.0 - coh / jnp.maximum(jnp.sqrt(inv), coh)) * relax
        mean = (field[0] + field[1] + field[2]) * (1.0 / 3.0)
        for q in range(3):
            emit(q, mean + factor * (field[q] - mean))
        for q in range(3, 6):
            emit(q, factor * field[q])
        for q in range(6, nq):
            emit(q, field[q])

    fine_relax = 1.0 - math.exp(-step_time / relax_time)
    coarse_relax = 1.0 - math.exp(-2.0 * step_time / relax_time)

    mats[...] = jnp.zeros_like(mats)
    for n in early:
        loads[n].wait()
    ng = project.shape[0]
    for d in range(3):
        mats[d * nb_ : (d + 1) * nb_, 0:nb_] = stiff[d]
        mats[rows + d * nb_ : rows + (d + 1) * nb_, 0:nb_] = stiff[d].T
    for f in range(nf):
        at = 2 * rows + f * gp
        mats[at : at + ng, 0:nb_] = project[:, f, :]
    high, low = parts(mats[...])
    a_mat[...] = jnp.concatenate([high, low, high], axis=1).astype(bf16)
    for d in range(3):
        send_s[d * nsub : (d + 1) * nsub, :] = send_rows[d].astype(f32)

    def later_constants():
        lift_t[...] = jnp.zeros_like(lift_t)
        for f in range(nf):
            lift_t[f * gp : f * gp + ng, :] = lift[:, f, :]
        high, low = parts(lift_t[...])
        first = jnp.concatenate([high, high], axis=0)
        second = jnp.concatenate([low, jnp.zeros_like(low)], axis=0)
        l_mat[...] = jnp.concatenate([first.T, second.T], axis=0).astype(bf16)
        rot_s[...] = jnp.zeros_like(rot_s)
        for h in range(3):
            rot_s[h * gp : h * gp + ng, 0:ng] = rotate[h]
        high, low = parts(rot_s[...].T)
        blank = jnp.zeros((r_ref.shape[1] - 3 * gp, 3 * gp), f32)
        r_ref[...] = jnp.concatenate([high, low, high, blank], axis=0).T.astype(bf16)

    for q in range(nq):
        x = dofs[q]
        u0[:, lanes(q)] = x
        put_cat(q, x)
        acc1[:, lanes(q)] = wts[0] * x
        acc2[:, lanes(q)] = wts[ORDER] * x
    series(True)
    copies = traces(0)
    for n in range(len(loads)):
        if n not in early:
            loads[n].wait()
    later_constants()
    for f in range(nf):
        code = face_source[f : f + 1, :]
        for r in range(0, nf * ne + rl, 32):
            row = lax.broadcasted_iota(jnp.int32, (32, ne), 0) + r
            hit = jnp.where(row == code, 1.0, 0.0).astype(bf16)
            if r < nf * ne:
                oh[r : r + 32, lanes(f)] = hit
            else:
                at = r - nf * ne
                far[at : at + 32, lanes(f)] = hit
                far[rl + at : rl + at + 32, lanes(f)] = hit
    far_constants()

    def keep(q, x):
        upd[:, lanes(q)] = x

    volume(keep)
    own_side()
    near_side()
    lifted = other_side(0, copies)
    upd[...] = upd[...] - lifted

    def keep_stepped(q, x):
        u1[:, lanes(q)] = x
        put_cat(q, x)
        acc1[:, lanes(q)] = wts[0] * x

    plastic([u0[:, lanes(q)] + upd[:, lanes(q)] for q in range(nq)], fine_relax, keep_stepped)

    series(False)
    fine = cluster[...] == 0
    for q in range(nq):
        acc1[:, lanes(q)] = jnp.where(fine, acc1[:, lanes(q)], acc2[:, lanes(q)])
    copies = traces(1)

    def keep_second(q, x):
        at = lanes(q)
        u1[:, at] = x + jnp.where(fine, u1[:, at], u0[:, at] + upd[:, at])

    volume(keep_second)
    own_side()
    near_side()
    upd[...] = other_side(1, copies)

    def write(q, x):
        out[q] = x

    plastic(
        [u1[:, lanes(q)] - upd[:, lanes(q)] for q in range(nq)],
        jnp.where(fine, fine_relax, coarse_relax),
        write,
    )


def local(
    mesh,
    dofs,
    star,
    flux_own,
    flux_nbr,
    cohesion,
    cluster,
    face_source,
    orient,
    send_rows,
    stiffness,
    project,
    lift,
    rotate,
):
    nbas, nq, ne = dofs.shape
    nf, ng = project.shape[0], project.shape[1]
    nsub, ndom = mesh.shape["sub"], mesh.shape["dom"]
    bp = round_up(nbas, 16)
    gp = round_up(ng, 8)
    npd = round_up(nq * gp, 32)
    rp = round_up(3 * gp, 16)
    nrecv = 3 * nsub * 8
    rl = round_up(nrecv, 128)
    dims = (nbas, nq, ne, nf, nsub, ndom, bp, gp, npd)
    vmem = pl.BlockSpec(memory_space=pltpu.VMEM)
    wide = nq * ne
    args = (
        jnp.transpose(dofs, (1, 0, 2)),
        jnp.transpose(star, (1, 2, 0, 3)),
        jnp.transpose(flux_own, (1, 2, 0, 3)),
        jnp.transpose(flux_nbr, (1, 2, 0, 3)),
        cohesion.reshape(1, ne),
        cluster.reshape(1, ne),
        face_source,
        orient,
        send_rows.reshape(send_rows.shape[2:]),
        stiffness,
        jnp.transpose(project, (1, 0, 2)),
        jnp.transpose(lift, (2, 0, 1)),
        rotate,
    )
    result = pl.pallas_call(
        functools.partial(kernel, dims),
        out_shape=pltpu.VMEM((nq, nbas, ne), f32),
        in_specs=[pl.BlockSpec(memory_space=pltpu.HBM)] * len(args),
        out_specs=vmem,
        scratch_shapes=[pltpu.VMEM(x.shape, x.dtype) for x in args]
        + [
            pltpu.VMEM((6 * nbas + nf * gp, bp), f32),
            pltpu.VMEM((nf * gp, nbas), f32),
            pltpu.VMEM((3 * gp, gp), f32),
            pltpu.VMEM((3 * nsub, 8), f32),
            pltpu.VMEM((6 * nbas + nf * gp, 3 * bp), bf16),
            pltpu.VMEM((2 * nbas, 2 * nf * gp), bf16),
            pltpu.VMEM((3 * gp, rp), bf16),
            pltpu.VMEM((3 * bp, wide), bf16),
            pltpu.VMEM((3 * nbas, wide), f32),
            pltpu.VMEM((nbas, wide), f32),
            pltpu.VMEM((nbas, wide), f32),
            pltpu.VMEM((nbas, wide), f32),
            pltpu.VMEM((nbas, wide), f32),
            pltpu.VMEM((nbas, wide), f32),
            pltpu.VMEM((nf * gp, wide), f32),
            pltpu.VMEM((2 * npd, nf * ne), bf16),
            pltpu.VMEM((nf * ne, nf * ne), bf16),
            pltpu.VMEM((2 * rl, nf * ne), bf16),
            pltpu.VMEM((nq * nq * nf, ne), f32),
            pltpu.VMEM((nq * nq, rl), f32),
            pltpu.VMEM((8, rl), f32),
            pltpu.VMEM((2 * npd, nf * ne), f32),
            pltpu.VMEM((nf * gp, wide), f32),
            pltpu.VMEM((nf * gp, wide), f32),
            pltpu.VMEM((2 * nf * gp, wide), bf16),
            pltpu.VMEM((2, 3 * nsub, 8, npd), f32),
            pltpu.VMEM((2, 3 * nsub, 8, npd), f32),
            pltpu.SemaphoreType.DMA((2, 3 * nsub)),
            pltpu.SemaphoreType.DMA((2, 3 * nsub)),
            pltpu.SemaphoreType.DMA((len(args),)),
        ],
        compiler_params=pltpu.CompilerParams(
            collective_id=0, has_side_effects=True, vmem_limit_bytes=48 * 1024 * 1024
        ),
        name="window",
    )(*(pltpu.with_memory_space_constraint(x, pltpu.HBM) for x in args))
    return jnp.transpose(result, (1, 0, 2))


def solution(mesh):
    both = ("dom", "sub")
    placed = (
        P(None, None, both),
        P(None, None, None, both),
        P(None, None, None, both),
        P(None, None, None, both),
        P(both),
        P(both),
        P(None, both),
        P(None, both),
        P("dom", "sub", None, None, None),
        P(),
        P(),
        P(),
        P(),
    )
    return jax.shard_map(
        functools.partial(local, mesh),
        mesh=mesh,
        in_specs=placed,
        out_specs=P(None, None, both),
        check_vma=False,
    )
```

```python
import functools
import math

import jax
import jax.numpy as jnp
from jax import lax
from jax.experimental import pallas as pl
from jax.experimental.pallas import tpu as pltpu
from jax.sharding import PartitionSpec as P

ORDER = 6
step_time = 0.5
relax_time = 0.5
f32 = jnp.float32
bf16 = jnp.bfloat16
MESH = pl.DeviceIdType.MESH


def series_weights():
    first, second = [], []
    for k in range(ORDER):
        sign = (-1.0) ** k / math.factorial(k + 1)
        low, high = step_time ** (k + 1), (2.0 * step_time) ** (k + 1)
        first.append(sign * low)
        second.append(sign * (high - low))
    return first + second


def round_up(n, m):
    return -(-n // m) * m


def parts(x):
    high = x.astype(bf16).astype(f32)
    return high, x - high


def split_rows(x):
    high = x.astype(bf16)
    return high, (x - high.astype(f32)).astype(bf16)


def kernel(dims, *refs):
    count = 13
    loaded = refs[count + 1 : 2 * count + 1]
    body(dims, refs[:count], loaded, refs[-1], *loaded, refs[count], *refs[2 * count + 1 : -1])


def body(
    dims,
    given,
    loaded,
    load_sem,
    dofs,
    star,
    flux_own,
    flux_nbr,
    cohesion,
    cluster,
    face_source,
    orient,
    send_rows,
    stiff,
    project,
    lift,
    rotate,
    out,
    mats,
    lift_t,
    rot_s,
    send_s,
    chosen_ref,
    a_mat,
    l_mat,
    r_ref,
    cat,
    prod,
    past,
    u0,
    u1,
    acc1,
    acc2,
    upd,
    tr,
    tcat,
    oh,
    far,
    flat,
    g_far,
    code_far,
    pick,
    nb,
    terms,
    tcat3,
    send,
    recv,
    send_sem,
    recv_sem,
):
    nb_, nq, ne, nf, nsub, ndom, bp, gp, npd = dims
    rows = 3 * nb_
    nrecv = 3 * nsub * 8
    rl = round_up(nrecv, 128)
    dom, sub = lax.axis_index("dom"), lax.axis_index("sub")

    def peer(direction, k):
        return (
            lax.rem(dom + direction - 1 + ndom, ndom),
            lax.rem(sub + k, nsub),
        )

    links = [(d, k) for d in range(3) for k in range(nsub) if not (d == 1 and k == 0)]
    low = 1 - (2 * sub) // nsub
    far_first = []
    for r in range(nsub):
        place = low * (nsub - 1 - 2 * r) + r
        apart = lax.rem(place - sub + nsub, nsub)
        far_first += [(0, apart), (2, apart)]
        if r + 1 < nsub:
            far_first.append((1, low * (nsub - 2 * (r + 1)) + r + 1))
    barrier = pltpu.get_barrier_semaphore()
    for d, k in links:
        pl.semaphore_signal(barrier, inc=1, device_id=peer(d, k), device_id_type=MESH)

    loads = [
        pltpu.make_async_copy(source, place, load_sem.at[n])
        for n, (source, place) in enumerate(zip(given, loaded))
    ]
    early = (0, 1, 8, 9, 10)
    first_loads = (9, 10, 8, 0, 1)
    for n in list(first_loads) + [n for n in range(len(loads)) if n not in early]:
        loads[n].start()

    def lanes(q):
        return slice(q * ne, (q + 1) * ne)

    pad_rows = jnp.zeros((bp - nb_, ne), f32)

    def put_cat(q, x):
        high, low = split_rows(jnp.concatenate([x, pad_rows], axis=0))
        cat[0:bp, lanes(q)] = high
        cat[bp : 2 * bp, lanes(q)] = high
        cat[2 * bp : 3 * bp, lanes(q)] = low

    def star_mul(emit):
        for q0 in range(0, nq, 3):
            qs = range(q0, min(q0 + 3, nq))
            accs = [None] * len(qs)
            for d in range(3):
                for p in range(nq):
                    block = prod[d * nb_ : (d + 1) * nb_, lanes(p)]
                    for n, q in enumerate(qs):
                        term = block * star[p, q, d : d + 1, :]
                        accs[n] = term if accs[n] is None else accs[n] + term
            for n, q in enumerate(qs):
                emit(q, accs[n])

    wts = series_weights()

    def pick_weight(k, base):
        value = jnp.float32(wts[base + ORDER - 1])
        for n in range(1, ORDER - 1):
            value = jnp.where(k == n, jnp.float32(wts[base + n]), value)
        return value

    def mat_cat(low, high):
        return jnp.dot(a_mat[low:high, :], cat[...], preferred_element_type=f32)

    def series(second_too):
        def body(k, carry):
            for p in range(0, nq, 2):
                at = slice(p * ne, min(p + 2, nq) * ne)
                prod[:, at] = jnp.dot(
                    a_mat[0:rows, :], cat[:, at], preferred_element_type=f32
                )
            w1 = pick_weight(k, 0)

            def emit(q, x):
                put_cat(q, x)
                acc1[:, lanes(q)] = acc1[:, lanes(q)] + w1 * x
                if second_too:
                    past[k - 1, :, lanes(q)] = x

            star_mul(emit)
            return carry

        lax.fori_loop(1, ORDER, body, 0)

    nt = (((1,), (1,)), ((), ()))

    def exchange(phase):
        copies = []
        for d, k in far_first:
            target = peer(d, k)
            copies.append(
                pltpu.make_async_remote_copy(
                    src_ref=send.at[phase, d * nsub + target[1]],
                    dst_ref=recv.at[phase, (2 - d) * nsub + sub],
                    send_sem=send_sem.at[phase, d * nsub + k],
                    recv_sem=recv_sem.at[phase, (2 - d) * nsub + k],
                    device_id=target,
                    device_id_type=MESH,
                )
            )
        return copies

    def traces(phase):
        for q in range(nq):
            put_cat(q, acc1[:, lanes(q)])
        tr[...] = mat_cat(2 * rows, 2 * rows + nf * gp)
        for f in range(nf):
            own = [tr[f * gp : (f + 1) * gp, lanes(q)] for q in range(nq)]
            own.append(jnp.zeros((npd - nq * gp, ne), f32))
            high, low = split_rows(jnp.concatenate(own, axis=0))
            tcat[0:npd, lanes(f)] = high
            tcat[npd : 2 * npd, lanes(f)] = low
        chosen = chosen_ref[...]
        outgoing = lax.dot_general(
            chosen, tcat[0:npd, :], nt, preferred_element_type=f32
        ) + lax.dot_general(chosen, tcat[npd : 2 * npd, :], nt, preferred_element_type=f32)
        send[phase] = outgoing.reshape(3 * nsub, 8, npd)
        if phase == 0:
            pl.semaphore_wait(barrier, len(links))
        copies = exchange(phase)
        for copy in copies:
            copy.start()
        return copies

    def volume(emit):
        prod[...] = mat_cat(rows, 2 * rows)
        star_mul(emit)

    def flux(source, matrix, first):
        for f in range(nf):
            at = slice(f * gp, (f + 1) * gp)
            if first:
                accs = [None] * nq
            else:
                accs = [terms[at, lanes(q)] for q in range(nq)]
            for p in range(nq):
                block = source[at, lanes(p)]
                for q in range(nq):
                    term = block * matrix(p, q, f)
                    accs[q] = term if accs[q] is None else accs[q] + term
            for q in range(nq):
                terms[at, lanes(q)] = accs[q]

    def own_side():
        pick[...] = jnp.dot(tcat[...], oh[...], preferred_element_type=f32)
        flux(tr, lambda p, q, f: flux_own[p, q, f : f + 1, :], True)

    def choose(turned, code, at):
        part = turned[:, at]
        return jnp.where(
            code == 0,
            part[0:gp],
            jnp.where(code == 1, part[gp : 2 * gp], part[2 * gp : 3 * gp]),
        )

    def near_side():
        r_mat = r_ref[...]
        extra = jnp.zeros((r_mat.shape[1] - 3 * gp, nf * ne), f32)
        for q in range(nq):
            high = pick[q * gp : (q + 1) * gp, :]
            low = pick[npd + q * gp : npd + (q + 1) * gp, :]
            stacked = jnp.concatenate([high, high, low, extra], axis=0).astype(bf16)
            turned = jnp.dot(r_mat, stacked, preferred_element_type=f32)
            for f in range(nf):
                code = jnp.broadcast_to(orient[f : f + 1, :], (gp, ne))
                nb[f * gp : (f + 1) * gp, lanes(q)] = choose(turned, code, lanes(f))
        flux(nb, lambda p, q, f: flux_nbr[p, q, f : f + 1, :], False)

    def far_constants():
        for p in range(nq):
            for q in range(nq):
                at = (p * nq + q) * nf
                flat[at : at + nf, :] = flux_nbr[p, q]
        total, turn = None, None
        for f in range(nf):
            hit = far[0:rl, lanes(f)]
            high, low = split_rows(flat[pl.ds(f, nq * nq, stride=nf), :])
            taken = lax.dot_general(high, hit, nt, preferred_element_type=f32)
            taken = taken + lax.dot_general(low, hit, nt, preferred_element_type=f32)
            total = taken if total is None else total + taken
            code = jnp.broadcast_to(orient[f : f + 1, :], (8, ne)).astype(f32).astype(bf16)
            taken = lax.dot_general(code, hit, nt, preferred_element_type=f32)
            turn = taken if turn is None else turn + taken
        g_far[...] = total
        code_far[...] = turn

    def other_side(phase, copies):
        for copy in copies:
            copy.wait()
        recv[phase, pl.ds(nsub + sub, 1)] = send[phase, pl.ds(nsub + sub, 1)]
        arrived = recv[phase].reshape(nrecv, npd)
        if rl > nrecv:
            arrived = jnp.concatenate([arrived, jnp.zeros((rl - nrecv, npd), f32)], axis=0)
        arrived = arrived.T
        r_mat = r_ref[...]
        wide = jnp.concatenate([arrived[q * gp : (q + 1) * gp] for q in range(nq)], axis=1)
        high, low = parts(wide)
        extra = jnp.zeros((r_mat.shape[1] - 3 * gp, nq * rl), f32)
        stacked = jnp.concatenate([high, high, low, extra], axis=0).astype(bf16)
        turned = jnp.dot(r_mat, stacked, preferred_element_type=f32)
        code = jnp.broadcast_to(code_far[0:1, :], (gp, rl))
        blocks = [choose(turned, code, slice(p * rl, (p + 1) * rl)) for p in range(nq)]
        sums = []
        for q in range(nq):
            total = None
            for p in range(nq):
                term = blocks[p] * g_far[p * nq + q : p * nq + q + 1, :]
                total = term if total is None else total + term
            sums.append(total)
        sums.append(jnp.zeros((npd - nq * gp, rl), f32))
        high, low = split_rows(jnp.concatenate(sums, axis=0))
        spread = jnp.dot(
            jnp.concatenate([high, low], axis=1), far[...], preferred_element_type=f32
        )
        ng = nf * gp
        for q in range(nq):
            whole = jnp.concatenate(
                [
                    terms[f * gp : (f + 1) * gp, lanes(q)]
                    + spread[q * gp : (q + 1) * gp, lanes(f)]
                    for f in range(nf)
                ],
                axis=0,
            )
            high, low = split_rows(whole)
            tcat3[0:ng, lanes(q)] = high
            tcat3[ng : 2 * ng, lanes(q)] = low
        both = jnp.dot(l_mat[...], tcat3[...], preferred_element_type=f32)
        return both[0:nb_] + both[nb_ : 2 * nb_]

    def plastic(field, relax, emit):
        s = [field[q][0:1, :] for q in range(6)]
        pressure = (s[0] + s[1] + s[2]) / 3.0
        dx, dy, dz = s[0] - pressure, s[1] - pressure, s[2] - pressure
        inv = (
            0.5 * (dx * dx + dy * dy + dz * dz) + s[3] * s[3] + s[4] * s[4] + s[5] * s[5]
        )
        coh = cohesion[...]
        factor = 1.0 - (1.0 - coh / jnp.maximum(jnp.sqrt(inv), coh)) * relax
        mean = (field[0] + field[1] + field[2]) * (1.0 / 3.0)
        for q in range(3):
            emit(q, mean + factor * (field[q] - mean))
        for q in range(3, 6):
            emit(q, factor * field[q])
        for q in range(6, nq):
            emit(q, field[q])

    fine_relax = 1.0 - math.exp(-step_time / relax_time)
    coarse_relax = 1.0 - math.exp(-2.0 * step_time / relax_time)

    mats[...] = jnp.zeros_like(mats)
    for n in first_loads[:3]:
        loads[n].wait()
    ng = project.shape[0]
    for d in range(3):
        mats[d * nb_ : (d + 1) * nb_, 0:nb_] = stiff[d]
        mats[rows + d * nb_ : rows + (d + 1) * nb_, 0:nb_] = stiff[d].T
    for f in range(nf):
        at = 2 * rows + f * gp
        mats[at : at + ng, 0:nb_] = project[:, f, :]
    high, low = parts(mats[...])
    a_mat[...] = jnp.concatenate([high, low, high], axis=1).astype(bf16)
    for d in range(3):
        send_s[d * nsub : (d + 1) * nsub, :] = send_rows[d].astype(f32)
    spots = lax.broadcasted_iota(jnp.int32, (8, nf * ne), 1).astype(f32)
    columns = send_s[...].T
    chosen_ref[...] = jnp.concatenate(
        [
            jnp.where(spots == columns[:, c : c + 1], 1.0, 0.0)
            for c in range(3 * nsub)
        ],
        axis=0,
    ).astype(bf16)

    def later_constants():
        lift_t[...] = jnp.zeros_like(lift_t)
        for f in range(nf):
            lift_t[f * gp : f * gp + ng, :] = lift[:, f, :]
        high, low = parts(lift_t[...])
        first = jnp.concatenate([high, high], axis=0)
        second = jnp.concatenate([low, jnp.zeros_like(low)], axis=0)
        l_mat[...] = jnp.concatenate([first.T, second.T], axis=0).astype(bf16)
        rot_s[...] = jnp.zeros_like(rot_s)
        for h in range(3):
            rot_s[h * gp : h * gp + ng, 0:ng] = rotate[h]
        high, low = parts(rot_s[...].T)
        blank = jnp.zeros((r_ref.shape[1] - 3 * gp, 3 * gp), f32)
        r_ref[...] = jnp.concatenate([high, low, high, blank], axis=0).T.astype(bf16)

    loads[0].wait()
    for q in range(nq):
        x = dofs[q]
        u0[:, lanes(q)] = x
        put_cat(q, x)
        acc1[:, lanes(q)] = wts[0] * x
    loads[1].wait()
    series(True)
    copies = traces(0)
    for n in range(len(loads)):
        if n not in early:
            loads[n].wait()
    later_constants()
    for f in range(nf):
        code = face_source[f : f + 1, :]
        for r in range(0, nf * ne + rl, 32):
            row = lax.broadcasted_iota(jnp.int32, (32, ne), 0) + r
            hit = jnp.where(row == code, 1.0, 0.0).astype(bf16)
            if r < nf * ne:
                oh[r : r + 32, lanes(f)] = hit
            else:
                at = r - nf * ne
                far[at : at + 32, lanes(f)] = hit
                far[rl + at : rl + at + 32, lanes(f)] = hit
    far_constants()

    def keep(q, x):
        upd[:, lanes(q)] = x

    for q in range(nq):
        later = wts[ORDER] * u0[:, lanes(q)]
        for k in range(1, ORDER):
            later = later + wts[ORDER + k] * past[k - 1, :, lanes(q)]
        acc2[:, lanes(q)] = later
    volume(keep)
    own_side()
    near_side()
    lifted = other_side(0, copies)
    upd[...] = upd[...] - lifted

    def keep_stepped(q, x):
        u1[:, lanes(q)] = x
        put_cat(q, x)
        acc1[:, lanes(q)] = wts[0] * x

    plastic([u0[:, lanes(q)] + upd[:, lanes(q)] for q in range(nq)], fine_relax, keep_stepped)

    series(False)
    fine = cluster[...] == 0
    for q in range(nq):
        acc1[:, lanes(q)] = jnp.where(fine, acc1[:, lanes(q)], acc2[:, lanes(q)])
    copies = traces(1)

    def keep_second(q, x):
        at = lanes(q)
        u1[:, at] = x + jnp.where(fine, u1[:, at], u0[:, at] + upd[:, at])

    volume(keep_second)
    own_side()
    near_side()
    upd[...] = other_side(1, copies)

    def write(q, x):
        out[q] = x

    plastic(
        [u1[:, lanes(q)] - upd[:, lanes(q)] for q in range(nq)],
        jnp.where(fine, fine_relax, coarse_relax),
        write,
    )


def local(
    mesh,
    dofs,
    star,
    flux_own,
    flux_nbr,
    cohesion,
    cluster,
    face_source,
    orient,
    send_rows,
    stiffness,
    project,
    lift,
    rotate,
):
    nbas, nq, ne = dofs.shape
    nf, ng = project.shape[0], project.shape[1]
    nsub, ndom = mesh.shape["sub"], mesh.shape["dom"]
    bp = round_up(nbas, 16)
    gp = round_up(ng, 8)
    npd = round_up(nq * gp, 32)
    rp = round_up(3 * gp, 16)
    nrecv = 3 * nsub * 8
    rl = round_up(nrecv, 128)
    dims = (nbas, nq, ne, nf, nsub, ndom, bp, gp, npd)
    vmem = pl.BlockSpec(memory_space=pltpu.VMEM)
    wide = nq * ne
    args = (
        jnp.transpose(dofs, (1, 0, 2)),
        jnp.transpose(star, (1, 2, 0, 3)),
        jnp.transpose(flux_own, (1, 2, 0, 3)),
        jnp.transpose(flux_nbr, (1, 2, 0, 3)),
        cohesion.reshape(1, ne),
        cluster.reshape(1, ne),
        face_source,
        orient,
        send_rows.reshape(send_rows.shape[2:]),
        stiffness,
        jnp.transpose(project, (1, 0, 2)),
        jnp.transpose(lift, (2, 0, 1)),
        rotate,
    )
    result = pl.pallas_call(
        functools.partial(kernel, dims),
        out_shape=pltpu.VMEM((nq, nbas, ne), f32),
        in_specs=[pl.BlockSpec(memory_space=pltpu.HBM)] * len(args),
        out_specs=vmem,
        scratch_shapes=[pltpu.VMEM(x.shape, x.dtype) for x in args]
        + [
            pltpu.VMEM((6 * nbas + nf * gp, bp), f32),
            pltpu.VMEM((nf * gp, nbas), f32),
            pltpu.VMEM((3 * gp, gp), f32),
            pltpu.VMEM((3 * nsub, 8), f32),
            pltpu.VMEM((nrecv, nf * ne), bf16),
            pltpu.VMEM((6 * nbas + nf * gp, 3 * bp), bf16),
            pltpu.VMEM((2 * nbas, 2 * nf * gp), bf16),
            pltpu.VMEM((3 * gp, rp), bf16),
            pltpu.VMEM((3 * bp, wide), bf16),
            pltpu.VMEM((3 * nbas, wide), f32),
            pltpu.VMEM((ORDER - 1, nbas, wide), f32),
            pltpu.VMEM((nbas, wide), f32),
            pltpu.VMEM((nbas, wide), f32),
            pltpu.VMEM((nbas, wide), f32),
            pltpu.VMEM((nbas, wide), f32),
            pltpu.VMEM((nbas, wide), f32),
            pltpu.VMEM((nf * gp, wide), f32),
            pltpu.VMEM((2 * npd, nf * ne), bf16),
            pltpu.VMEM((nf * ne, nf * ne), bf16),
            pltpu.VMEM((2 * rl, nf * ne), bf16),
            pltpu.VMEM((nq * nq * nf, ne), f32),
            pltpu.VMEM((nq * nq, rl), f32),
            pltpu.VMEM((8, rl), f32),
            pltpu.VMEM((2 * npd, nf * ne), f32),
            pltpu.VMEM((nf * gp, wide), f32),
            pltpu.VMEM((nf * gp, wide), f32),
            pltpu.VMEM((2 * nf * gp, wide), bf16),
            pltpu.VMEM((2, 3 * nsub, 8, npd), f32),
            pltpu.VMEM((2, 3 * nsub, 8, npd), f32),
            pltpu.SemaphoreType.DMA((2, 3 * nsub)),
            pltpu.SemaphoreType.DMA((2, 3 * nsub)),
            pltpu.SemaphoreType.DMA((len(args),)),
        ],
        compiler_params=pltpu.CompilerParams(
            collective_id=0, has_side_effects=True, vmem_limit_bytes=48 * 1024 * 1024
        ),
        name="window",
    )(*(pltpu.with_memory_space_constraint(x, pltpu.HBM) for x in args))
    return jnp.transpose(result, (1, 0, 2))


def solution(mesh):
    both = ("dom", "sub")
    placed = (
        P(None, None, both),
        P(None, None, None, both),
        P(None, None, None, both),
        P(None, None, None, both),
        P(both),
        P(both),
        P(None, both),
        P(None, both),
        P("dom", "sub", None, None, None),
        P(),
        P(),
        P(),
        P(),
    )
    return jax.shard_map(
        functools.partial(local, mesh),
        mesh=mesh,
        in_specs=placed,
        out_specs=P(None, None, both),
        check_vma=False,
    )
```
